256 devices in a mesh: dp: 16 (over z, core), vocab: 16 (over x, y).
Axes of the slice: x: 4, y: 4, z: 8, core: 2. Of those that a mesh axis runs over, the one named last changes fastest.
Arguments:
- hidden: bfloat16 [4096, 4096], P('dp')
- table: bfloat16 [16384, 4096], P(('vocab', 'dp')), as said below
- targets: int32 [4096], P('dp'), may hold values from 0 to 16383
- token_scale: float32 [4096], P('dp'), may hold values from 2 to 32
- enc_ids: int32 [4096], P(('dp', 'vocab')), may hold values from 0 to 16383
- enc_cot: bfloat16 [4096, 4096], P(('dp', 'vocab')), may hold values from -6 to 6
- dec_ids: int32 [4096], P(('dp', 'vocab')), may hold values from 0 to 16383
- dec_cot: bfloat16 [4096, 4096], P(('dp', 'vocab')), may hold values from -6 to 6
Outputs:
- grad_hidden: bfloat16 [4096, 4096], P('dp', 'vocab')
- grad_table: float32 [16384, 4096], P(('vocab', 'dp'))
- loss: float32 [4096], P('dp')
The draws below stay inside these ranges and needn't reach their ends.
Inputs may be any that keep to these rules, and one draw needn't show every extreme that they name: table entries of order 3 / sqrt(4096).
All inputs are finite; a program needn't handle non-finite values.
Results may differ from the reference program's by a relative error of at most 0.018.
Values may be sent and summed in bfloat16 or wider, within the bound.
No kernel may reach another device: no remote copies, remote signals or barrier semaphores. Data moves between devices by JAX's collectives and lax.ppermute only.
A program may use at most 128 MiB of HBM per device.

```python
import math
import jax
import jax.numpy as jnp
import numpy as np
from jax import lax

D = 4096
V = 16384
TOK_DEV = 256
IDS_DEV = 16
TOKENS = 4096
IDS = 4096
N_DP = 16
N_VOCAB = 16


def shared_table(key):
    noise = jax.random.normal(jax.random.fold_in(key, 11), (V, D), jnp.float32)
    return jnp.clip(noise, -4.0, 4.0) * (3.0 / D ** 0.5)


def draw_table(key, part):
    return shared_table(key).astype(jnp.bfloat16)


def draw_hidden(key, part):
    return jax.random.normal(jax.random.fold_in(key, 12), (TOKENS, D), jnp.float32).astype(jnp.bfloat16)


def plant(values, stream_key, low, high):
    dims = values.shape
    spot = [jax.random.randint(jax.random.fold_in(stream_key, axis), (), 0, dims[axis]) for axis in range(len(dims))]
    values = values.at[tuple(spot)].set(low)
    longest = dims.index(max(dims))
    spot[longest] = (spot[longest] + 1) % dims[longest]
    return values.at[tuple(spot)].set(high)


def level_of(stream_key, extent, shards, least, top_value):
    factor_of, own = 1.0, jax.random.fold_in(stream_key, 6)
    for position, shards_of in shards:
        heights = jnp.exp(jax.random.uniform(jax.random.fold_in(own, position), (shards_of,), jnp.float32, least / len(shards), top_value / len(shards)))
        factor_of = factor_of * jnp.repeat(heights, extent[position] // shards_of).reshape([-1 if axis == position else 1 for axis in range(len(extent))])
    return factor_of


def cumulative_ranks(amount, lean):
    portions = [(1 << 20) // math.isqrt(standing ** lean) + 1 for standing in range(1, amount + 1)]
    deviation = 1 + sum(portions) // (1 << 30)
    return np.cumsum(np.array([max(1, weight // deviation) for weight in portions]))


def ranked(key, dims, amount, skew):
    table = cumulative_ranks(amount, skew)
    pick = jax.random.randint(jax.random.fold_in(key, 1), dims, 0, int(table[amount - 1]))
    standing = jnp.searchsorted(jnp.asarray(table, jnp.int32), pick, side="right")
    return jax.random.permutation(jax.random.fold_in(key, 2), amount)[standing].astype(jnp.int32)


def bell_draw(stream_key, dims, width, most, cuts=(), kind=jnp.bfloat16):
    values = jax.random.normal(stream_key, dims, jnp.float32) * width
    if len(cuts) > 0:
        values = level_of(stream_key, dims, cuts, -0.22, 0.18) * values
    return jnp.clip(values, min=-most, max=most).astype(kind)


def setup_inputs(seed: int = 0) -> dict:
    keys = jax.random.split(jax.random.key(seed), 9)
    hidden = draw_hidden(jax.random.fold_in(keys[8], 71), 0)
    table = draw_table(jax.random.fold_in(keys[8], 71), 0)
    targets = plant(ranked(keys[2], (TOKENS,), V, 2), jax.random.fold_in(keys[2], 3), 0, V - 1).astype(jnp.int32)
    token_scale = jnp.clip(jnp.exp(math.log(32.0) - 2.7725887 * jax.random.uniform(keys[3], (TOKENS,), jnp.float32) ** level_of(keys[3], (TOKENS,), ((0, 16),), -0.2, 0.2)), 2.0, 32.0)
    enc_ids = plant(ranked(keys[4], (IDS,), V, 2), jax.random.fold_in(keys[4], 3), 0, V - 1).astype(jnp.int32)
    enc_cot = bell_draw(keys[5], (IDS, D), 1.0, 6.0, ((0, 256),))
    dec_ids = plant(ranked(keys[6], (IDS,), V, 3), jax.random.fold_in(keys[6], 3), 0, V - 1).astype(jnp.int32)
    dec_cot = bell_draw(keys[7], (IDS, D), 1.0, 6.0, ((0, 256),))
    return {"hidden": hidden, "table": table, "targets": targets, "token_scale": token_scale, "enc_ids": enc_ids, "enc_cot": enc_cot, "dec_ids": dec_ids, "dec_cot": dec_cot}


def reference(hidden, table, targets, token_scale, enc_ids, enc_cot, dec_ids, dec_cot):
    group_ids = IDS_DEV * N_VOCAB

    def one_group(total, index):
        rows = (index * TOK_DEV).astype(jnp.int32)
        id_start = (index * group_ids).astype(jnp.int32)
        states = lax.dynamic_slice_in_dim(hidden, rows, TOK_DEV, 0)
        wanted = lax.dynamic_slice_in_dim(targets, rows, TOK_DEV, 0)
        scales = lax.dynamic_slice_in_dim(token_scale, rows, TOK_DEV, 0)
        logits = jnp.dot(states, table.T, preferred_element_type=jnp.float32)
        row_max = jnp.max(logits, axis=1)
        expo = jnp.exp(logits - row_max[:, None])
        row_sum = jnp.sum(expo, axis=1)
        target_logit = jnp.take_along_axis(logits, wanted[:, None], axis=1)[:, 0]
        loss = row_max + jnp.log(row_sum) - target_logit
        matches = (jnp.arange(V, dtype=jnp.int32)[None, :] == wanted[:, None]).astype(jnp.float32)
        dlogits = (scales[:, None] * (expo / row_sum[:, None] - matches)).astype(jnp.bfloat16)
        grad_states = jnp.dot(dlogits, table, preferred_element_type=jnp.float32).astype(jnp.bfloat16)
        head = jnp.dot(dlogits.T, states, preferred_element_type=jnp.float32)
        ids_one = lax.dynamic_slice_in_dim(enc_ids, id_start, group_ids, 0)
        cot_one = lax.dynamic_slice_in_dim(enc_cot, id_start, group_ids, 0).astype(jnp.float32)
        ids_two = lax.dynamic_slice_in_dim(dec_ids, id_start, group_ids, 0)
        cot_two = lax.dynamic_slice_in_dim(dec_cot, id_start, group_ids, 0).astype(jnp.float32)
        head = head.at[ids_one].add(cot_one).at[ids_two].add(cot_two)
        rounded = lax.optimization_barrier(head.astype(jnp.bfloat16))
        return total + rounded.astype(jnp.float32), (grad_states, loss)

    start = jnp.zeros((V, D), jnp.float32)
    total, (grad_parts, loss_parts) = lax.scan(one_group, start, jnp.arange(N_DP, dtype=jnp.int32))
    grad_hidden = grad_parts.reshape(TOKENS, D)
    loss = loss_parts.reshape(TOKENS)
    return grad_hidden, total, loss
```

```python
import jax
import jax.numpy as jnp
from jax import lax
from jax.sharding import Mesh, PartitionSpec as P

bf16, f32 = jnp.bfloat16, jnp.float32


def shift(x, axis, k):
    n = lax.axis_size(axis)
    return lax.ppermute(x, axis, [(i, (i + k) % n) for i in range(n)])


def swap(x):
    return lax.ppermute(x, "c", [(0, 1), (1, 0)])


def pair(x):
    other = swap(x)
    first = lax.axis_index("c") == 0
    return jnp.concatenate([jnp.where(first, x, other), jnp.where(first, other, x)], 0)


def ring_scatter(piece, axis, width):
    half = width // 2
    far = piece(2)
    up = shift(far[:, :half], axis, 1)
    down = shift(far[:, half:], axis, -1)
    one, minus = piece(1).astype(f32), piece(-1).astype(f32)
    up = jnp.concatenate([up.astype(f32) + one[:, :half], one[:, half:]], 1)
    down = jnp.concatenate([minus[:, :half], down.astype(f32) + minus[:, half:]], 1)
    up = shift(up.astype(bf16), axis, 1)
    down = shift(down.astype(bf16), axis, -1)
    return (piece(0).astype(f32) + up + down).astype(bf16)


def shards(hidden, table, targets, token_scale, enc_ids, enc_cot, dec_ids, dec_cot):
    rows, depth = table.shape
    z, c = lax.axis_index("z"), lax.axis_index("c")
    x, y = lax.axis_index("x"), lax.axis_index("y")
    nz = lax.axis_size("z")
    base = (x * lax.axis_size("y") + y) * (rows * nz * 2)

    cots = lax.all_gather(
        jnp.concatenate([enc_cot, dec_cot], 0), ("c", "x", "y"), axis=0, tiled=True
    )
    ids = jnp.concatenate([enc_ids, dec_ids], 0)
    n_peers = 2 * lax.axis_size("x") * lax.axis_size("y")
    ids = lax.all_to_all(
        jnp.broadcast_to(ids[None], (n_peers, ids.shape[0])),
        ("c", "x", "y"), 0, 0, tiled=True,
    ).reshape(-1)

    half = rows // 2
    blocks = {0: table}
    up, down = table, table
    for k in range(1, nz // 2):
        up = shift(up, "z", 1)
        down = shift(down, "z", -1)
        blocks[-k], blocks[k] = up, down
    far_up = shift(up[:half], "z", 1)
    far_down = shift(down[half:], "z", -1)
    blocks[nz // 2] = jnp.concatenate([far_up, far_down], 0)

    states = pair(hidden)
    wanted = pair(targets)
    scales = pair(token_scale)

    order = [[0]] + [[-k, k] for k in range(1, nz // 2)] + [[nz // 2]]
    groups = [
        jnp.concatenate([blocks[k] for k in group], 0) if len(group) > 1 else blocks[group[0]]
        for group in order
    ]
    row_ids = [
        jnp.concatenate(
            [base + ((z + k + nz) % nz * 2 + c) * rows + jnp.arange(rows, dtype=jnp.int32) for k in group]
        )
        for group in order
    ]
    logits = jnp.concatenate(
        [
            lax.dot_general(states, g, (((1,), (1,)), ((), ())), preferred_element_type=f32)
            for g in groups
        ],
        1,
    )
    columns = jnp.concatenate(row_ids)
    matches = columns[None, :] == wanted[:, None]
    local_max = jnp.max(logits, axis=1)
    local_sum = jnp.sum(jnp.exp(logits - local_max[:, None]), axis=1)
    local_target = jnp.sum(jnp.where(matches, logits, 0.0), axis=1)
    stats = jnp.stack([local_max, local_sum, local_target])
    stats = lax.all_to_all(
        jnp.broadcast_to(stats[None], (n_peers,) + stats.shape),
        ("c", "x", "y"), 0, 0, tiled=True,
    )
    row_max = jnp.max(stats[:, 0], axis=0)
    row_sum = jnp.sum(stats[:, 1] * jnp.exp(stats[:, 0] - row_max), axis=0)
    target_logit = jnp.sum(stats[:, 2], axis=0)
    loss = row_max + jnp.log(row_sum) - target_logit
    tokens = hidden.shape[0]
    loss = lax.dynamic_slice_in_dim(loss, c * tokens, tokens, 0)
    dlogits = (
        scales[:, None]
        * (jnp.exp(logits - row_max[:, None]) / row_sum[:, None] - matches.astype(f32))
    ).astype(bf16)

    heads, start = {}, 0
    starts = []
    for group in order:
        starts.append(start)
        start += rows * len(group)
    for group, begin, names in list(zip(order, starts, row_ids))[::-1]:
        width = rows * len(group)
        hits = (names[:, None] == ids[None, :]).astype(bf16)
        term = lax.dot_general(
            dlogits[:, begin : begin + width], states, (((0,), (0,)), ((), ())),
            preferred_element_type=f32,
        ) + jnp.dot(hits, cots, preferred_element_type=f32)
        for i, k in enumerate(group):
            heads[k] = term[i * rows : (i + 1) * rows]
    mid = depth // 2
    far = heads[nz // 2].astype(bf16)
    up = shift(far[:, :mid], "z", 1)
    down = shift(far[:, mid:], "z", -1)
    for k in range(nz // 2 - 1, 0, -1):
        if up.shape[1] == mid:
            up = jnp.concatenate([heads[k][:, :mid] + up, heads[k][:, mid:]], 1)
            down = jnp.concatenate([heads[-k][:, :mid], heads[-k][:, mid:] + down], 1)
        else:
            up, down = heads[k] + up, heads[-k] + down
        up = shift(up.astype(bf16), "z", 1)
        down = shift(down.astype(bf16), "z", -1)
    grad_table = heads[0] + up.astype(f32) + down.astype(f32)

    gathered = jnp.concatenate(groups, 0)
    own = lax.dynamic_slice_in_dim(dlogits, c * tokens, tokens, 0)
    theirs = lax.dynamic_slice_in_dim(dlogits, (1 - c) * tokens, tokens, 0)
    given = swap(jnp.dot(theirs, gathered, preferred_element_type=f32).astype(bf16))
    state_term = (jnp.dot(own, gathered, preferred_element_type=f32) + given).astype(bf16)
    nx, ny = lax.axis_size("x"), lax.axis_size("y")
    wx = depth // nx
    part = ring_scatter(
        lambda k: lax.dynamic_slice_in_dim(state_term, (x + k + nx) % nx * wx, wx, 1), "x", wx
    )
    wy = wx // ny
    grad_hidden = ring_scatter(
        lambda k: lax.dynamic_slice_in_dim(part, (y + k + ny) % ny * wy, wy, 1), "y", wy
    )
    return (grad_hidden, grad_table, loss)


def solution(mesh):
    fine = Mesh(mesh.devices.reshape(8, 2, 4, 4), ("z", "c", "x", "y"))
    dp, vocab, every = ("z", "c"), ("x", "y"), ("z", "c", "x", "y")
    return jax.shard_map(
        shards,
        mesh=fine,
        in_specs=(
            P(dp, None), P(vocab + dp, None), P(dp), P(dp),
            P(every), P(every, None), P(every), P(every, None),
        ),
        out_specs=(P(dp, vocab), P(vocab + dp, None), P(dp)),
        check_vma=False,
    )
```

```python
import jax
import jax.numpy as jnp
from jax import lax
from jax.experimental import pallas as pl
from jax.experimental.pallas import tpu as pltpu
from jax.sharding import Mesh, PartitionSpec as P

bf16, f32, i32 = jnp.bfloat16, jnp.float32, jnp.int32
NX, NY, NZ = 4, 4, 8
PARAMS = pltpu.CompilerParams(vmem_limit_bytes=40 << 20)
ALONE = pltpu.CompilerParams(vmem_limit_bytes=60 << 20)


def shift(x, k):
    return lax.ppermute(x, "z", [(i, (i + k) % NZ) for i in range(NZ)])


def swap(x):
    return lax.ppermute(x, "c", [(0, 1), (1, 0)])


def after(x, *others):
    return lax.optimization_barrier((x,) + others)[0]


def legs(leg):
    groups = []
    for c in range(2):
        for i in range(4):
            places = [(j, i) if c == leg else (i, j) for j in range(4)]
            groups.append([(c * NX + x) * NY + y for x, y in places])
    return groups


def exchange(x, leg):
    return lax.all_to_all(
        x, ("c", "x", "y"), 0, 0, axis_index_groups=legs(leg), tiled=True
    )


def cost(flops, moved):
    return pl.CostEstimate(flops=flops, bytes_accessed=moved, transcendentals=0)


def stats_body(logits_ref, names_ref, wanted_ref, out_ref):
    logits = logits_ref[...]
    top = jnp.max(logits, axis=0, keepdims=True)
    out_ref[0:1] = top
    out_ref[1:2] = jnp.sum(jnp.exp(logits - top), axis=0, keepdims=True)
    hit = names_ref[...] == wanted_ref[...]
    out_ref[2:3] = jnp.sum(jnp.where(hit, logits, 0.0), axis=0, keepdims=True)


def head_body(
    starts, logits_ref, names_ref, tokens_ref, wanted_ref, in_order_ref, ids_ref,
    own_ref, other_ref, cots_ref, out_ref, d_ref, sorted_ref, hits_ref,
):
    @pl.when(pl.program_id(0) == 0)
    def _():
        rows = d_ref.shape[0] // NZ
        share = jnp.exp(logits_ref[...] - tokens_ref[0:1]) / tokens_ref[1:2]
        hit = (names_ref[...] == wanted_ref[...]).astype(f32)
        d_ref[...] = (tokens_ref[2:3] * (share - hit)).astype(bf16)
        for k in range(NZ):
            start = pl.multiple_of(starts[k], rows)
            sorted_ref[pl.ds(start, rows), :] = d_ref[k * rows : (k + 1) * rows]
        hits_ref[...] = (in_order_ref[...] == ids_ref[...]).astype(f32).astype(bf16)

    tokens = own_ref.shape[0]
    term = jnp.dot(hits_ref[...], cots_ref[...], preferred_element_type=f32)
    term += jnp.dot(sorted_ref[:, :tokens], own_ref[...], preferred_element_type=f32)
    term += jnp.dot(sorted_ref[:, tokens:], other_ref[...], preferred_element_type=f32)
    out_ref[...] = term.astype(bf16)


def state_body(order, d_ref, *refs):
    *table_refs, own_ref, their_ref, turned = refs

    @pl.when(pl.program_id(0) == 0)
    def _():
        turned[...] = d_ref[...].astype(f32).T.astype(bf16)

    start, term = 0, 0.0
    for t_ref in table_refs:
        stop = start + t_ref.shape[0]
        term += jnp.dot(turned[:, start:stop], t_ref[...], preferred_element_type=f32)
        start = stop
    tokens = own_ref.shape[1]
    own_ref[0] = term[:tokens].astype(bf16)
    their_ref[0] = term[tokens:].astype(bf16)


def shards(hidden, table, targets, token_scale, enc_ids, enc_cot, dec_ids, dec_cot):
    rows, depth = table.shape
    tokens = hidden.shape[0]
    vocab = rows * NZ
    z, c = lax.axis_index("z"), lax.axis_index("c")
    x, y = lax.axis_index("x"), lax.axis_index("y")
    base = (x * NY + y) * (vocab * 2)

    ids = jnp.concatenate([enc_ids, dec_ids])
    lane = lax.broadcasted_iota(i32, (ids.shape[0], 128), 1)
    tail = jnp.where(
        lane == 0, (ids // 128)[:, None], jnp.where(lane == 1, (ids % 128)[:, None], 0)
    ).astype(bf16)
    cots = jnp.concatenate([jnp.concatenate([enc_cot, dec_cot], 0), tail], 1)
    cots = lax.all_gather(cots, ("c", "x", "y"), axis=0, tiled=True)
    ids = cots[:, depth : depth + 2].astype(i32)
    ids = (ids[:, 0] * 128 + ids[:, 1])[None]
    n_ids = ids.shape[1]
    peers = 2 * NX * NY

    half = rows // 2
    up, down = shift(table, 1), shift(table, -1)
    blocks = {0: table, -1: up, 1: down}
    other, wanted, scales = swap(hidden), swap(targets), swap(token_scale)
    wanted = jnp.concatenate([targets, wanted])[None]
    scales = jnp.concatenate([token_scale, scales])[None]
    for k in range(2, NZ // 2):
        up, down = lax.optimization_barrier((up, down, other, wanted, scales))[:2]
        up, down = shift(up, 1), shift(down, -1)
        blocks[-k], blocks[k] = up, down
    up, down = shift(up[:half], 1), shift(down[half:], -1)
    blocks[NZ // 2] = jnp.concatenate([up, down], 0)

    order = [[0, 1, -1, 2], [-2, 3, -3], [NZ // 2]]
    parts = [jnp.concatenate([blocks[k] for k in g], 0) for g in order]
    parts = [lax.optimization_barrier(part) for part in parts]
    states = jnp.concatenate([hidden, other], 0)
    logits = jnp.concatenate(
        [
            lax.dot_general(g, states, (((1,), (1,)), ((), ())), preferred_element_type=f32)
            for g in parts
        ],
        0,
    )
    places = jnp.array([k for g in order for k in g], i32)
    places = (z + places + NZ) % NZ
    spread = jnp.arange(rows, dtype=i32)
    names = ((base + (places * 2 + c) * rows)[:, None] + spread).reshape(vocab, 1)
    in_order = ((base + (jnp.arange(NZ, dtype=i32) * 2 + c) * rows)[:, None] + spread).reshape(vocab, 1)

    stats = pl.pallas_call(
        stats_body,
        out_shape=jax.ShapeDtypeStruct((3, 2 * tokens), f32),
        compiler_params=PARAMS,
        cost_estimate=cost(8 * vocab * tokens, 8 * vocab * tokens),
        name="stats",
    )(logits, names, wanted)
    turned = jnp.concatenate([stats[:, tokens:], stats[:, :tokens]], 1)
    stats = jnp.where(jnp.arange(2)[:, None, None] == c, stats[None], turned[None])
    stats = jnp.broadcast_to(stats[:, None], (2, NX * NY) + stats.shape[1:])
    stats = lax.all_to_all(
        stats.reshape((peers,) + stats.shape[2:]), ("c", "x", "y"), 0, 0, tiled=True
    )

    row_max = jnp.max(stats[:, 0], axis=0)
    row_sum = jnp.sum(stats[:, 1] * jnp.exp(stats[:, 0] - row_max), axis=0)
    loss = row_max + jnp.log(row_sum) - jnp.sum(stats[:, 2], axis=0)

    width = 512
    head, dlogits = pl.pallas_call(
        head_body,
        out_shape=(
            jax.ShapeDtypeStruct((vocab, depth), bf16),
            jax.ShapeDtypeStruct((vocab, 2 * tokens), bf16),
        ),
        grid_spec=pltpu.PrefetchScalarGridSpec(
            num_scalar_prefetch=1,
            grid=(depth // width,),
            in_specs=[
                pl.BlockSpec((vocab, 2 * tokens), lambda i, s: (0, 0)),
                pl.BlockSpec((vocab, 1), lambda i, s: (0, 0)),
                pl.BlockSpec((3, 2 * tokens), lambda i, s: (0, 0)),
                pl.BlockSpec((1, 2 * tokens), lambda i, s: (0, 0)),
                pl.BlockSpec((vocab, 1), lambda i, s: (0, 0)),
                pl.BlockSpec((1, n_ids), lambda i, s: (0, 0)),
                pl.BlockSpec((tokens, width), lambda i, s: (0, i)),
                pl.BlockSpec((tokens, width), lambda i, s: (0, i)),
                pl.BlockSpec((n_ids, width), lambda i, s: (0, i)),
            ],
            out_specs=(
                pl.BlockSpec((vocab, width), lambda i, s: (0, i)),
                pl.BlockSpec((vocab, 2 * tokens), lambda i, s: (0, 0)),
            ),
            scratch_shapes=[
                pltpu.VMEM((vocab, 2 * tokens), bf16),
                pltpu.VMEM((vocab, n_ids), bf16),
            ],
        ),
        compiler_params=ALONE,
        cost_estimate=cost(
            2 * vocab * (2 * tokens + n_ids) * depth, 2 * (vocab + 2 * tokens + n_ids) * depth
        ),
        name="head",
    )(
        places * rows, logits, names, jnp.concatenate([row_max[None], row_sum[None], scales]),
        wanted, in_order, ids, hidden, other, cots,
    )
    grad_table = lax.psum_scatter(head, "z", scatter_dimension=0, tiled=True).astype(f32)

    width = depth // (NX * NY)
    spot = jnp.arange(NX * NY, dtype=i32)
    spot = jnp.where(c == 0, spot, spot % 4 * 4 + spot // 4)
    out = pl.BlockSpec((1, tokens, width), lambda i, order: (i // 4, 0, i % 4))
    given = pl.BlockSpec((1, tokens, width), lambda i, order: (i % 4, 0, i // 4))
    own, theirs = pl.pallas_call(
        state_body,
        out_shape=(jax.ShapeDtypeStruct((4, tokens, depth // 4), bf16),) * 2,
        grid_spec=pltpu.PrefetchScalarGridSpec(
            num_scalar_prefetch=1,
            grid=(NX * NY,),
            in_specs=[
                pl.BlockSpec((vocab, 2 * tokens), lambda i, order: (0, 0)),
            ]
            + [pl.BlockSpec((p.shape[0], width), lambda i, order: (0, order[i])) for p in parts],
            out_specs=(out, given),
            scratch_shapes=[pltpu.VMEM((2 * tokens, vocab), bf16)],
        ),
        compiler_params=PARAMS,
        cost_estimate=cost(4 * vocab * tokens * depth, 2 * (vocab + 2 * tokens) * depth),
        name="state_terms",
    )(spot, dlogits, *parts)
    term = (own.astype(f32) + swap(theirs).astype(f32)).astype(bf16)
    term = jnp.sum(exchange(term, 0).astype(f32), 0)
    term = jnp.stack([term[:, i * width : (i + 1) * width] for i in range(4)]).astype(bf16)
    grad_hidden = jnp.sum(exchange(term, 1).astype(f32), 0).astype(bf16)
    return (grad_hidden, grad_table, loss[:tokens])


def solution(mesh):
    fine = Mesh(mesh.devices.reshape(NZ, 2, NX, NY), ("z", "c", "x", "y"))
    dp, vocab, every = ("z", "c"), ("x", "y"), ("z", "c", "x", "y")
    return jax.shard_map(
        shards,
        mesh=fine,
        in_specs=(
            P(dp, None), P(vocab + dp, None), P(dp), P(dp),
            P(every), P(every, None), P(every), P(every, None),
        ),
        out_specs=(P(dp, vocab), P(vocab + dp, None), P(dp)),
        check_vma=False,
    )
```

```python
import jax
import jax.numpy as jnp
from jax import lax
from jax.experimental import pallas as pl
from jax.experimental.pallas import tpu as pltpu
from jax.sharding import Mesh, PartitionSpec as P

bf16, f32, i32 = jnp.bfloat16, jnp.float32, jnp.int32
NX, NY, NZ = 4, 4, 8
PARAMS = pltpu.CompilerParams(vmem_limit_bytes=40 << 20)
ANY = pl.BlockSpec(memory_space=pl.ANY)
VMEM = pl.BlockSpec(memory_space=pltpu.VMEM)
SMEM = pl.BlockSpec(memory_space=pltpu.SMEM)
WIDTH = 512
ALONE = pltpu.CompilerParams(vmem_limit_bytes=60 << 20)


def shift(x, k):
    return lax.ppermute(x, "z", [(i, (i + k) % NZ) for i in range(NZ)])


def swap(x):
    return lax.ppermute(x, "c", [(0, 1), (1, 0)])


def after(x, *others):
    return lax.optimization_barrier((x,) + others)[0]


def legs(leg):
    groups = []
    for c in range(2):
        for i in range(4):
            places = [(j, i) if c == leg else (i, j) for j in range(4)]
            groups.append([(c * NX + x) * NY + y for x, y in places])
    return groups


def exchange(x, leg):
    return lax.all_to_all(
        x, ("c", "x", "y"), 0, 0, axis_index_groups=legs(leg), tiled=True
    )


def cost(flops, moved):
    return pl.CostEstimate(flops=flops, bytes_accessed=moved, transcendentals=0)


def stats_body(logits_ref, names_ref, wanted_ref, out_ref):
    logits = logits_ref[...]
    top = jnp.max(logits, axis=0, keepdims=True)
    out_ref[0:1] = top
    out_ref[1:2] = jnp.sum(jnp.exp(logits - top), axis=0, keepdims=True)
    hit = names_ref[...] == wanted_ref[...]
    out_ref[2:3] = jnp.sum(jnp.where(hit, logits, 0.0), axis=0, keepdims=True)


def columns(ref, i):
    return ref.at[:, pl.ds(i * WIDTH, WIDTH)]


def lookup_body(names_ref, ids_ref, cots_hbm, out_hbm, hits, cots_ref, sums, in_sems, out_sems):
    steps = out_hbm.shape[1] // WIDTH

    def fetch(i):
        return pltpu.make_async_copy(columns(cots_hbm, i), columns(cots_ref, i), in_sems.at[i])

    def store(i):
        return pltpu.make_async_copy(sums.at[i % 2], columns(out_hbm, i), out_sems.at[i % 2])

    for i in range(steps):
        fetch(i).start()
    hits[...] = (names_ref[...] == ids_ref[...]).astype(f32).astype(bf16)
    for i in range(steps):
        fetch(i).wait()
        if i >= 2:
            store(i - 2).wait()
        cols = slice(i * WIDTH, (i + 1) * WIDTH)
        term = jnp.dot(hits[...], cots_ref[:, cols], preferred_element_type=f32)
        sums[i % 2] = term.astype(bf16)
        store(i).start()
    store(steps - 2).wait()
    store(steps - 1).wait()


def head_body(
    starts, logits_ref, names_ref, tokens_ref, wanted_ref, own_hbm, other_hbm, looked_hbm,
    out_hbm, d_ref, sorted_ref, own_ref, other_ref, looked_ref, sums, in_sems, out_sems,
):
    steps = out_hbm.shape[1] // WIDTH

    def fetches(i):
        pairs = ((own_hbm, own_ref), (other_hbm, other_ref), (looked_hbm, looked_ref))
        return [
            pltpu.make_async_copy(columns(src, i), columns(dst, i), in_sems.at[j, i])
            for j, (src, dst) in enumerate(pairs)
        ]

    def store(i):
        return pltpu.make_async_copy(sums.at[i % 2], columns(out_hbm, i), out_sems.at[i % 2])

    for i in range(steps):
        for fetch in fetches(i):
            fetch.start()
    share = jnp.exp(logits_ref[...] - tokens_ref[0:1]) / tokens_ref[1:2]
    hit = (names_ref[...] == wanted_ref[...]).astype(f32)
    d_ref[...] = (tokens_ref[2:3] * (share - hit)).astype(bf16)
    pieces = starts.shape[0]
    rows = d_ref.shape[0] // pieces
    for k in range(pieces):
        start = pl.multiple_of(starts[k], rows)
        sorted_ref[pl.ds(start, rows), :] = d_ref[k * rows : (k + 1) * rows]

    tokens = own_ref.shape[0]
    for i in range(steps):
        for fetch in fetches(i):
            fetch.wait()
        cols = slice(i * WIDTH, (i + 1) * WIDTH)
        term = looked_ref[:, cols].astype(f32)
        term += jnp.dot(sorted_ref[:, :tokens], own_ref[:, cols], preferred_element_type=f32)
        term += jnp.dot(sorted_ref[:, tokens:], other_ref[:, cols], preferred_element_type=f32)
        if i >= 2:
            store(i - 2).wait()
        sums[i % 2] = term.astype(bf16)
        store(i).start()
    store(steps - 2).wait()
    store(steps - 1).wait()


def state_body(order, d_ref, *refs):
    n = (len(refs) - 4) // 2
    table_hbm, own_ref, their_ref, turned = refs[:n], refs[n], refs[n + 1], refs[n + 2]
    table_refs, sems = refs[n + 3 : -1], refs[-1]
    tokens, width = own_ref.shape[1], own_ref.shape[2] // 4

    def fetches(i):
        cols = pl.ds(i * WIDTH, WIDTH)
        return [
            pltpu.make_async_copy(src.at[:, cols], dst.at[:, cols], sems.at[j, i])
            for j, (src, dst) in enumerate(zip(table_hbm, table_refs))
        ]

    steps = table_hbm[0].shape[1] // WIDTH
    for i in range(steps):
        for fetch in fetches(i):
            fetch.start()
    turned[...] = d_ref[...].astype(f32).T.astype(bf16)
    for i in range(steps):
        for fetch in fetches(i):
            fetch.wait()
        start, term = 0, 0.0
        for t_ref in table_refs:
            stop = start + t_ref.shape[0]
            part = t_ref[:, i * WIDTH : (i + 1) * WIDTH]
            term += jnp.dot(turned[:, start:stop], part, preferred_element_type=f32)
            start = stop
        for j in range(WIDTH // width):
            spot = order[i * (WIDTH // width) + j]
            one, two = spot // 4, spot % 4
            block = term[:, j * width : (j + 1) * width].astype(bf16)
            own_ref[one, :, pl.ds(pl.multiple_of(two * width, width), width)] = block[:tokens]
            their_ref[two, :, pl.ds(pl.multiple_of(one * width, width), width)] = block[tokens:]


def shards(hidden, table, targets, token_scale, enc_ids, enc_cot, dec_ids, dec_cot):
    rows, depth = table.shape
    tokens = hidden.shape[0]
    vocab = rows * NZ
    z, c = lax.axis_index("z"), lax.axis_index("c")
    x, y = lax.axis_index("x"), lax.axis_index("y")
    base = (x * NY + y) * (vocab * 2)

    ids = jnp.concatenate([enc_ids, dec_ids])
    lane = lax.broadcasted_iota(i32, (ids.shape[0], 128), 1)
    tail = jnp.where(
        lane == 0, (ids // 128)[:, None], jnp.where(lane == 1, (ids % 128)[:, None], 0)
    ).astype(bf16)
    cots = jnp.concatenate([jnp.concatenate([enc_cot, dec_cot], 0), tail], 1)
    cots = lax.all_gather(cots, ("c", "x", "y"), axis=0, tiled=True)
    ids = cots[:, depth : depth + 2].astype(i32)
    ids = (ids[:, 0] * 128 + ids[:, 1])[None]
    n_ids = ids.shape[1]
    peers = 2 * NX * NY

    half = rows // 2
    up, down = shift(table, 1), shift(table, -1)
    blocks = {0: table, -1: up, 1: down}
    other, wanted, scales = swap(hidden), swap(targets), swap(token_scale)
    wanted = jnp.concatenate([targets, wanted])[None]
    scales = jnp.concatenate([token_scale, scales])[None]
    for k in range(2, NZ // 2):
        up, down = lax.optimization_barrier((up, down, other, wanted, scales))[:2]
        up, down = shift(up, 1), shift(down, -1)
        blocks[-k], blocks[k] = up, down
    up, down = shift(up[:half], 1), shift(down[half:], -1)
    blocks[NZ // 2] = jnp.concatenate([up, down], 0)

    order = [[0, 1, -1, 2], [-2, 3, -3], [NZ // 2]]
    parts = [jnp.concatenate([blocks[k] for k in g], 0) for g in order]
    parts = [lax.optimization_barrier(part) for part in parts]
    states = jnp.concatenate([hidden, other], 0)
    logits = jnp.concatenate(
        [
            lax.dot_general(g, states, (((1,), (1,)), ((), ())), preferred_element_type=f32)
            for g in parts
        ],
        0,
    )
    places = jnp.array([k for g in order for k in g], i32)
    places = (z + places + NZ) % NZ
    spread = jnp.arange(rows, dtype=i32)
    names = ((base + (places * 2 + c) * rows)[:, None] + spread).reshape(vocab, 1)
    in_order = ((base + (jnp.arange(NZ, dtype=i32) * 2 + c) * rows)[:, None] + spread).reshape(vocab, 1)

    stats = pl.pallas_call(
        stats_body,
        out_shape=jax.ShapeDtypeStruct((3, 2 * tokens), f32),
        compiler_params=PARAMS,
        cost_estimate=cost(8 * vocab * tokens, 8 * vocab * tokens),
        name="stats",
    )(logits, names, wanted)
    turned = jnp.concatenate([stats[:, tokens:], stats[:, :tokens]], 1)
    stats = jnp.where(jnp.arange(2)[:, None, None] == c, stats[None], turned[None])
    stats = jnp.broadcast_to(stats[:, None], (2, NX * NY) + stats.shape[1:])
    stats = lax.all_to_all(
        stats.reshape((peers,) + stats.shape[2:]), ("c", "x", "y"), 0, 0, tiled=True
    )

    looked_up = pl.pallas_call(
        lookup_body,
        out_shape=jax.ShapeDtypeStruct((vocab, depth), bf16),
        in_specs=[VMEM, VMEM, ANY],
        out_specs=ANY,
        scratch_shapes=[
            pltpu.VMEM((vocab, n_ids), bf16),
            pltpu.VMEM((n_ids, depth), bf16),
            pltpu.VMEM((2, vocab, WIDTH), bf16),
            pltpu.SemaphoreType.DMA((depth // WIDTH,)),
            pltpu.SemaphoreType.DMA((2,)),
        ],
        compiler_params=ALONE,
        cost_estimate=cost(2 * vocab * n_ids * depth, 2 * n_ids * depth + 2 * vocab * depth),
        name="lookup",
    )(in_order, ids, cots)
    stats, looked_up = lax.optimization_barrier((stats, looked_up))
    row_max = jnp.max(stats[:, 0], axis=0)
    row_sum = jnp.sum(stats[:, 1] * jnp.exp(stats[:, 0] - row_max), axis=0)
    loss = row_max + jnp.log(row_sum) - jnp.sum(stats[:, 2], axis=0)

    head, dlogits = pl.pallas_call(
        head_body,
        out_shape=(
            jax.ShapeDtypeStruct((vocab, depth), bf16),
            jax.ShapeDtypeStruct((vocab, 2 * tokens), bf16),
        ),
        in_specs=[SMEM] + [VMEM] * 4 + [ANY] * 3,
        out_specs=(ANY, VMEM),
        scratch_shapes=[
            pltpu.VMEM((vocab, 2 * tokens), bf16),
            pltpu.VMEM((tokens, depth), bf16),
            pltpu.VMEM((tokens, depth), bf16),
            pltpu.VMEM((vocab, depth), bf16),
            pltpu.VMEM((2, vocab, WIDTH), bf16),
            pltpu.SemaphoreType.DMA((3, depth // WIDTH)),
            pltpu.SemaphoreType.DMA((2,)),
        ],
        compiler_params=ALONE,
        cost_estimate=cost(4 * vocab * tokens * depth, 4 * vocab * depth + 4 * tokens * depth),
        name="head",
    )(
        places * rows, logits, names, jnp.concatenate([row_max[None], row_sum[None], scales]),
        wanted, hidden, other, looked_up,
    )
    grad_table = lax.psum_scatter(head, "z", scatter_dimension=0, tiled=True).astype(f32)

    width = depth // (NX * NY)
    spot = jnp.arange(NX * NY, dtype=i32)
    spot = jnp.where(c == 0, spot, spot % 4 * 4 + spot // 4)
    own, theirs = pl.pallas_call(
        state_body,
        out_shape=(jax.ShapeDtypeStruct((4, tokens, depth // 4), bf16),) * 2,
        in_specs=[SMEM, VMEM] + [ANY] * len(parts),
        out_specs=(VMEM, VMEM),
        scratch_shapes=[pltpu.VMEM((2 * tokens, vocab), bf16)]
        + [pltpu.VMEM(part.shape, bf16) for part in parts]
        + [pltpu.SemaphoreType.DMA((len(parts), depth // WIDTH))],
        compiler_params=PARAMS,
        cost_estimate=cost(4 * vocab * tokens * depth, 2 * (vocab + 2 * tokens) * depth),
        name="state_terms",
    )(spot, dlogits, *parts)
    term = (own.astype(f32) + swap(theirs).astype(f32)).astype(bf16)
    term = jnp.sum(exchange(term, 0).astype(f32), 0)
    term = jnp.stack([term[:, i * width : (i + 1) * width] for i in range(4)]).astype(bf16)
    grad_hidden = jnp.sum(exchange(term, 1).astype(f32), 0).astype(bf16)
    return (grad_hidden, grad_table, loss[:tokens])


def solution(mesh):
    fine = Mesh(mesh.devices.reshape(NZ, 2, NX, NY), ("z", "c", "x", "y"))
    dp, vocab, every = ("z", "c"), ("x", "y"), ("z", "c", "x", "y")
    return jax.shard_map(
        shards,
        mesh=fine,
        in_specs=(
            P(dp, None), P(vocab + dp, None), P(dp), P(dp),
            P(every), P(every, None), P(every), P(every, None),
        ),
        out_specs=(P(dp, vocab), P(vocab + dp, None), P(dp)),
        check_vma=False,
    )
```

```python
import jax
import jax.numpy as jnp
from jax import lax
from jax.experimental import pallas as pl
from jax.experimental.pallas import tpu as pltpu
from jax.sharding import Mesh, PartitionSpec as P

bf16, f32, i32 = jnp.bfloat16, jnp.float32, jnp.int32
NX, NY, NZ = 4, 4, 8
PARAMS = pltpu.CompilerParams(vmem_limit_bytes=40 << 20)
ANY = pl.BlockSpec(memory_space=pl.ANY)
VMEM = pl.BlockSpec(memory_space=pltpu.VMEM)
SMEM = pl.BlockSpec(memory_space=pltpu.SMEM)
WIDTH = 512
ALONE = pltpu.CompilerParams(vmem_limit_bytes=60 << 20)


def shift(x, k):
    return lax.ppermute(x, "z", [(i, (i + k) % NZ) for i in range(NZ)])


def swap(x):
    return lax.ppermute(x, "c", [(0, 1), (1, 0)])


def after(x, *others):
    return lax.optimization_barrier((x,) + others)[0]


def legs(leg):
    groups = []
    for c in range(2):
        for i in range(4):
            places = [(j, i) if c == leg else (i, j) for j in range(4)]
            groups.append([(c * NX + x) * NY + y for x, y in places])
    return groups


def exchange(x, leg):
    return lax.all_to_all(
        x, ("c", "x", "y"), 0, 0, axis_index_groups=legs(leg), tiled=True
    )


def cost(flops, moved):
    return pl.CostEstimate(flops=flops, bytes_accessed=moved, transcendentals=0)


def gather_body(enc_ids_ref, dec_ids_ref, enc_ref, dec_ref, out_ref):
    n, depth = enc_ref.shape
    row = lax.broadcasted_iota(i32, (n, n), 0)
    same = row == lax.broadcasted_iota(i32, (n, n), 1)
    lane = lax.broadcasted_iota(i32, (n, 128), 1)
    for i, (ids_ref, rows_ref) in enumerate(((enc_ids_ref, enc_ref), (dec_ids_ref, dec_ref))):
        out_ref[i * n : (i + 1) * n, :depth] = rows_ref[...]
        ids = jnp.sum(jnp.where(same, ids_ref[...], 0), axis=1, keepdims=True)
        tail = jnp.where(lane == 0, ids >> 7, jnp.where(lane == 1, ids & 127, 0))
        out_ref[i * n : (i + 1) * n, depth:] = tail.astype(f32).astype(bf16)


def stats_body(logits_ref, names_ref, wanted_ref, out_ref):
    logits = logits_ref[...]
    top = jnp.max(logits, axis=0, keepdims=True)
    out_ref[0:1] = top
    out_ref[1:2] = jnp.sum(jnp.exp(logits - top), axis=0, keepdims=True)
    hit = names_ref[...] == wanted_ref[...]
    out_ref[2:3] = jnp.sum(jnp.where(hit, logits, 0.0), axis=0, keepdims=True)


def columns(ref, i):
    return ref.at[:, pl.ds(i * WIDTH, WIDTH)]


def lookup_body(names_ref, cots_hbm, out_hbm, hits, cots_ref, tail_ref, sums, in_sems, out_sems):
    steps = out_hbm.shape[1] // WIDTH

    def fetch(i):
        return pltpu.make_async_copy(columns(cots_hbm, i), columns(cots_ref, i), in_sems.at[i])

    def store(i):
        return pltpu.make_async_copy(sums.at[i % 2], columns(out_hbm, i), out_sems.at[i % 2])

    tail = pltpu.make_async_copy(
        cots_hbm.at[:, pl.ds(steps * WIDTH, 128)], tail_ref, in_sems.at[steps]
    )
    tail.start()
    for i in range(steps):
        fetch(i).start()
    tail.wait()
    ids = tail_ref[...].astype(f32).T
    ids = ids[0:1] * 128.0 + ids[1:2]
    hits[...] = (names_ref[...].astype(f32) == ids).astype(f32).astype(bf16)
    for i in range(steps):
        fetch(i).wait()
        if i >= 2:
            store(i - 2).wait()
        cols = slice(i * WIDTH, (i + 1) * WIDTH)
        term = jnp.dot(hits[...], cots_ref[:, cols], preferred_element_type=f32)
        sums[i % 2] = term.astype(bf16)
        store(i).start()
    store(steps - 2).wait()
    store(steps - 1).wait()


def head_body(
    starts, logits_ref, names_ref, tokens_ref, wanted_ref, own_hbm, other_hbm, looked_hbm,
    out_hbm, d_ref, sorted_ref, own_ref, other_ref, looked_ref, sums, in_sems, out_sems,
):
    steps = out_hbm.shape[1] // WIDTH

    def fetches(i):
        pairs = ((own_hbm, own_ref), (other_hbm, other_ref), (looked_hbm, looked_ref))
        return [
            pltpu.make_async_copy(columns(src, i), columns(dst, i), in_sems.at[j, i])
            for j, (src, dst) in enumerate(pairs)
        ]

    def store(i):
        return pltpu.make_async_copy(sums.at[i % 2], columns(out_hbm, i), out_sems.at[i % 2])

    for i in range(steps):
        for fetch in fetches(i):
            fetch.start()
    share = jnp.exp(logits_ref[...] - tokens_ref[0:1]) * (1.0 / tokens_ref[1:2])
    hit = (names_ref[...] == wanted_ref[...]).astype(f32)
    d_ref[...] = (tokens_ref[2:3] * (share - hit)).astype(bf16)
    pieces = starts.shape[0]
    rows = d_ref.shape[0] // pieces
    for k in range(pieces):
        start = pl.multiple_of(starts[k], rows)
        sorted_ref[pl.ds(start, rows), :] = d_ref[k * rows : (k + 1) * rows]

    tokens = own_ref.shape[0]
    for i in range(steps):
        for fetch in fetches(i):
            fetch.wait()
        cols = slice(i * WIDTH, (i + 1) * WIDTH)
        term = looked_ref[:, cols].astype(f32)
        term += jnp.dot(sorted_ref[:, :tokens], own_ref[:, cols], preferred_element_type=f32)
        term += jnp.dot(sorted_ref[:, tokens:], other_ref[:, cols], preferred_element_type=f32)
        if i >= 2:
            store(i - 2).wait()
        sums[i % 2] = term.astype(bf16)
        store(i).start()
    store(steps - 2).wait()
    store(steps - 1).wait()


def state_body(order, d_ref, *refs):
    n = (len(refs) - 4) // 2
    table_hbm, own_ref, their_ref, turned = refs[:n], refs[n], refs[n + 1], refs[n + 2]
    table_refs, sems = refs[n + 3 : -1], refs[-1]
    tokens, width = own_ref.shape[1], own_ref.shape[2] // 4

    def fetches(i):
        cols = pl.ds(i * WIDTH, WIDTH)
        return [
            pltpu.make_async_copy(src.at[:, cols], dst.at[:, cols], sems.at[j, i])
            for j, (src, dst) in enumerate(zip(table_hbm, table_refs))
        ]

    steps = table_hbm[0].shape[1] // WIDTH
    for i in range(steps):
        for fetch in fetches(i):
            fetch.start()
    turned[...] = d_ref[...].astype(f32).T.astype(bf16)
    for i in range(steps):
        for fetch in fetches(i):
            fetch.wait()
        start, term = 0, 0.0
        for t_ref in table_refs:
            stop = start + t_ref.shape[0]
            part = t_ref[:, i * WIDTH : (i + 1) * WIDTH]
            term += jnp.dot(turned[:, start:stop], part, preferred_element_type=f32)
            start = stop
        for j in range(WIDTH // width):
            spot = order[i * (WIDTH // width) + j]
            one, two = spot // 4, spot % 4
            block = term[:, j * width : (j + 1) * width].astype(bf16)
            own_ref[one, :, pl.ds(pl.multiple_of(two * width, width), width)] = block[:tokens]
            their_ref[two, :, pl.ds(pl.multiple_of(one * width, width), width)] = block[tokens:]


def shards(hidden, table, targets, token_scale, enc_ids, enc_cot, dec_ids, dec_cot):
    rows, depth = table.shape
    tokens = hidden.shape[0]
    vocab = rows * NZ
    z, c = lax.axis_index("z"), lax.axis_index("c")
    x, y = lax.axis_index("x"), lax.axis_index("y")
    base = (x * NY + y) * (vocab * 2)

    cots = pl.pallas_call(
        gather_body,
        out_shape=jax.ShapeDtypeStruct((2 * enc_cot.shape[0], depth + 128), bf16),
        compiler_params=ALONE,
        name="id_rows",
    )(enc_ids[None], dec_ids[None], enc_cot, dec_cot)
    cots = lax.all_gather(cots, ("c", "x", "y"), axis=0, tiled=True)
    n_ids = cots.shape[0]
    peers = 2 * NX * NY

    half = rows // 2
    up, down = shift(table, 1), shift(table, -1)
    blocks = {0: table, -1: up, 1: down}
    other, wanted, scales = swap(hidden), swap(targets), swap(token_scale)
    wanted = jnp.concatenate([targets, wanted])[None]
    scales = jnp.concatenate([token_scale, scales])[None]
    for k in range(2, NZ // 2):
        up, down = lax.optimization_barrier((up, down, other, wanted, scales))[:2]
        up, down = shift(up, 1), shift(down, -1)
        blocks[-k], blocks[k] = up, down
    up, down = shift(up[:half], 1), shift(down[half:], -1)
    blocks[NZ // 2] = jnp.concatenate([up, down], 0)

    order = [[0, 1, -1, 2], [-2, 3, -3], [NZ // 2]]
    parts = [jnp.concatenate([blocks[k] for k in g], 0) for g in order]
    parts = [lax.optimization_barrier(part) for part in parts]
    states = jnp.concatenate([hidden, other], 0)
    logits = jnp.concatenate(
        [
            lax.dot_general(g, states, (((1,), (1,)), ((), ())), preferred_element_type=f32)
            for g in parts
        ],
        0,
    )
    places = jnp.array([k for g in order for k in g], i32)
    places = (z + places + NZ) % NZ
    spread = jnp.arange(rows, dtype=i32)
    names = ((base + (places * 2 + c) * rows)[:, None] + spread).reshape(vocab, 1)
    in_order = ((base + (jnp.arange(NZ, dtype=i32) * 2 + c) * rows)[:, None] + spread).reshape(vocab, 1)

    stats = pl.pallas_call(
        stats_body,
        out_shape=jax.ShapeDtypeStruct((3, 2 * tokens), f32),
        compiler_params=PARAMS,
        cost_estimate=cost(8 * vocab * tokens, 8 * vocab * tokens),
        name="stats",
    )(logits, names, wanted)
    turned = jnp.concatenate([stats[:, tokens:], stats[:, :tokens]], 1)
    stats = jnp.where(jnp.arange(2)[:, None, None] == c, stats[None], turned[None])
    stats = jnp.broadcast_to(stats[:, None], (2, NX * NY) + stats.shape[1:])
    stats = lax.all_to_all(
        stats.reshape((peers,) + stats.shape[2:]), ("c", "x", "y"), 0, 0, tiled=True
    )

    looked_up = pl.pallas_call(
        lookup_body,
        out_shape=jax.ShapeDtypeStruct((vocab, depth), bf16),
        in_specs=[VMEM, ANY],
        out_specs=ANY,
        scratch_shapes=[
            pltpu.VMEM((vocab, n_ids), bf16),
            pltpu.VMEM((n_ids, depth), bf16),
            pltpu.VMEM((n_ids, 128), bf16),
            pltpu.VMEM((2, vocab, WIDTH), bf16),
            pltpu.SemaphoreType.DMA((depth // WIDTH + 1,)),
            pltpu.SemaphoreType.DMA((2,)),
        ],
        compiler_params=ALONE,
        cost_estimate=cost(2 * vocab * n_ids * depth, 2 * n_ids * depth + 2 * vocab * depth),
        name="lookup",
    )(in_order, cots)
    stats, looked_up = lax.optimization_barrier((stats, looked_up))
    row_max = jnp.max(stats[:, 0], axis=0)
    row_sum = jnp.sum(stats[:, 1] * jnp.exp(stats[:, 0] - row_max), axis=0)
    loss = row_max + jnp.log(row_sum) - jnp.sum(stats[:, 2], axis=0)

    head, dlogits = pl.pallas_call(
        head_body,
        out_shape=(
            jax.ShapeDtypeStruct((vocab, depth), bf16),
            jax.ShapeDtypeStruct((vocab, 2 * tokens), bf16),
        ),
        in_specs=[SMEM] + [VMEM] * 4 + [ANY] * 3,
        out_specs=(ANY, VMEM),
        scratch_shapes=[
            pltpu.VMEM((vocab, 2 * tokens), bf16),
            pltpu.VMEM((tokens, depth), bf16),
            pltpu.VMEM((tokens, depth), bf16),
            pltpu.VMEM((vocab, depth), bf16),
            pltpu.VMEM((2, vocab, WIDTH), bf16),
            pltpu.SemaphoreType.DMA((3, depth // WIDTH)),
            pltpu.SemaphoreType.DMA((2,)),
        ],
        compiler_params=ALONE,
        cost_estimate=cost(4 * vocab * tokens * depth, 4 * vocab * depth + 4 * tokens * depth),
        name="head",
    )(
        places * rows, logits, names, jnp.concatenate([row_max[None], row_sum[None], scales]),
        wanted, hidden, other, looked_up,
    )
    grad_table = lax.psum_scatter(head, "z", scatter_dimension=0, tiled=True).astype(f32)

    width = depth // (NX * NY)
    spot = jnp.arange(NX * NY, dtype=i32)
    spot = jnp.where(c == 0, spot, spot % 4 * 4 + spot // 4)
    own, theirs = pl.pallas_call(
        state_body,
        out_shape=(jax.ShapeDtypeStruct((4, tokens, depth // 4), bf16),) * 2,
        in_specs=[SMEM, VMEM] + [ANY] * len(parts),
        out_specs=(VMEM, VMEM),
        scratch_shapes=[pltpu.VMEM((2 * tokens, vocab), bf16)]
        + [pltpu.VMEM(part.shape, bf16) for part in parts]
        + [pltpu.SemaphoreType.DMA((len(parts), depth // WIDTH))],
        compiler_params=PARAMS,
        cost_estimate=cost(4 * vocab * tokens * depth, 2 * (vocab + 2 * tokens) * depth),
        name="state_terms",
    )(spot, dlogits, *parts)
    term = (own.astype(f32) + swap(theirs).astype(f32)).astype(bf16)
    term = jnp.sum(exchange(term, 0).astype(f32), 0)
    term = jnp.stack([term[:, i * width : (i + 1) * width] for i in range(4)]).astype(bf16)
    grad_hidden = jnp.sum(exchange(term, 1).astype(f32), 0).astype(bf16)
    return (grad_hidden, grad_table, loss[:tokens])


def solution(mesh):
    fine = Mesh(mesh.devices.reshape(NZ, 2, NX, NY), ("z", "c", "x", "y"))
    dp, vocab, every = ("z", "c"), ("x", "y"), ("z", "c", "x", "y")
    return jax.shard_map(
        shards,
        mesh=fine,
        in_specs=(
            P(dp, None), P(vocab + dp, None), P(dp), P(dp),
            P(every), P(every, None), P(every), P(every, None),
        ),
        out_specs=(P(dp, vocab), P(vocab + dp, None), P(dp)),
        check_vma=False,
    )
```

```python
import jax
import jax.numpy as jnp
from jax import lax
from jax.experimental import pallas as pl
from jax.experimental.pallas import tpu as pltpu
from jax.sharding import Mesh, PartitionSpec as P

bf16, f32, i32 = jnp.bfloat16, jnp.float32, jnp.int32
NX, NY, NZ = 4, 4, 8
PARAMS = pltpu.CompilerParams(vmem_limit_bytes=40 << 20)
ANY = pl.BlockSpec(memory_space=pl.ANY)
VMEM = pl.BlockSpec(memory_space=pltpu.VMEM)
SMEM = pl.BlockSpec(memory_space=pltpu.SMEM)
WIDTH = 512
ALONE = pltpu.CompilerParams(vmem_limit_bytes=60 << 20)


def shift(x, k):
    return lax.ppermute(x, "z", [(i, (i + k) % NZ) for i in range(NZ)])


def swap(x):
    return lax.ppermute(x, "c", [(0, 1), (1, 0)])


def after(x, *others):
    return lax.optimization_barrier((x,) + others)[0]


def legs(leg):
    groups = []
    for c in range(2):
        for i in range(4):
            places = [(j, i) if c == leg else (i, j) for j in range(4)]
            groups.append([(c * NX + x) * NY + y for x, y in places])
    return groups


def exchange(x, leg):
    return lax.all_to_all(
        x, ("c", "x", "y"), 0, 0, axis_index_groups=legs(leg), tiled=True
    )


def cost(flops, moved):
    return pl.CostEstimate(flops=flops, bytes_accessed=moved, transcendentals=0)


def gather_body(enc_ids_ref, dec_ids_ref, enc_ref, dec_ref, out_ref):
    n, depth = enc_ref.shape
    row = lax.broadcasted_iota(i32, (n, n), 0)
    same = row == lax.broadcasted_iota(i32, (n, n), 1)
    lane = lax.broadcasted_iota(i32, (n, 128), 1)
    for i, (ids_ref, rows_ref) in enumerate(((enc_ids_ref, enc_ref), (dec_ids_ref, dec_ref))):
        out_ref[i * n : (i + 1) * n, :depth] = rows_ref[...]
        ids = jnp.sum(jnp.where(same, ids_ref[...], 0), axis=1, keepdims=True)
        tail = jnp.where(lane == 0, ids >> 7, jnp.where(lane == 1, ids & 127, 0))
        out_ref[i * n : (i + 1) * n, depth:] = tail.astype(f32).astype(bf16)


def stats_body(core, logits_ref, names_ref, wanted_ref, out_ref):
    logits = logits_ref[...]
    top = jnp.max(logits, axis=0, keepdims=True)
    total = jnp.sum(jnp.exp(logits - top), axis=0, keepdims=True)
    hit = names_ref[...] == wanted_ref[...]
    target = jnp.sum(jnp.where(hit, logits, 0.0), axis=0, keepdims=True)
    peers, tokens = out_ref.shape[0] // 2, out_ref.shape[2] // 2
    for i, value in enumerate((top, total, target)):
        turned = jnp.concatenate([value[:, tokens:], value[:, :tokens]], 1)
        for c in range(2):
            message = jnp.where(core[0] == c, value, turned)
            for j in range(peers):
                out_ref[c * peers + j, i : i + 1] = message


def columns(ref, i):
    return ref.at[:, pl.ds(i * WIDTH, WIDTH)]


def lookup_body(names_ref, cots_hbm, out_hbm, hits, cots_ref, tail_ref, sums, in_sems, out_sems):
    steps = out_hbm.shape[1] // WIDTH

    def fetch(i):
        return pltpu.make_async_copy(columns(cots_hbm, i), columns(cots_ref, i), in_sems.at[i])

    def store(i):
        return pltpu.make_async_copy(sums.at[i % 2], columns(out_hbm, i), out_sems.at[i % 2])

    tail = pltpu.make_async_copy(
        cots_hbm.at[:, pl.ds(steps * WIDTH, 128)], tail_ref, in_sems.at[steps]
    )
    tail.start()
    for i in range(steps):
        fetch(i).start()
    tail.wait()
    ids = tail_ref[...].astype(f32).T
    ids = ids[0:1] * 128.0 + ids[1:2]
    hits[...] = (names_ref[...].astype(f32) == ids).astype(f32).astype(bf16)
    for i in range(steps):
        fetch(i).wait()
        if i >= 2:
            store(i - 2).wait()
        cols = slice(i * WIDTH, (i + 1) * WIDTH)
        term = jnp.dot(hits[...], cots_ref[:, cols], preferred_element_type=f32)
        sums[i % 2] = term.astype(bf16)
        store(i).start()
    store(steps - 2).wait()
    store(steps - 1).wait()


def head_body(
    starts, logits_ref, names_ref, tokens_ref, wanted_ref, own_hbm, other_hbm, looked_hbm,
    out_hbm, d_ref, sorted_ref, own_ref, other_ref, looked_ref, sums, in_sems, out_sems,
):
    steps = out_hbm.shape[1] // WIDTH

    def fetches(i):
        pairs = ((own_hbm, own_ref), (other_hbm, other_ref), (looked_hbm, looked_ref))
        return [
            pltpu.make_async_copy(columns(src, i), columns(dst, i), in_sems.at[j, i])
            for j, (src, dst) in enumerate(pairs)
        ]

    def store(i):
        return pltpu.make_async_copy(sums.at[i % 2], columns(out_hbm, i), out_sems.at[i % 2])

    for i in range(steps):
        for fetch in fetches(i):
            fetch.start()
    share = jnp.exp(logits_ref[...] - tokens_ref[0:1]) * (1.0 / tokens_ref[1:2])
    hit = (names_ref[...] == wanted_ref[...]).astype(f32)
    d_ref[...] = (tokens_ref[2:3] * (share - hit)).astype(bf16)
    pieces = starts.shape[0]
    rows = d_ref.shape[0] // pieces
    for k in range(pieces):
        start = pl.multiple_of(starts[k], rows)
        sorted_ref[pl.ds(start, rows), :] = d_ref[k * rows : (k + 1) * rows]

    tokens = own_ref.shape[0]
    for i in range(steps):
        for fetch in fetches(i):
            fetch.wait()
        cols = slice(i * WIDTH, (i + 1) * WIDTH)
        term = looked_ref[:, cols].astype(f32)
        term += jnp.dot(sorted_ref[:, :tokens], own_ref[:, cols], preferred_element_type=f32)
        term += jnp.dot(sorted_ref[:, tokens:], other_ref[:, cols], preferred_element_type=f32)
        if i >= 2:
            store(i - 2).wait()
        sums[i % 2] = term.astype(bf16)
        store(i).start()
    store(steps - 2).wait()
    store(steps - 1).wait()


def state_body(order, d_ref, *refs):
    n = (len(refs) - 4) // 2
    table_hbm, own_ref, their_ref, turned = refs[:n], refs[n], refs[n + 1], refs[n + 2]
    table_refs, sems = refs[n + 3 : -1], refs[-1]
    tokens, width = own_ref.shape[1], own_ref.shape[2] // 4

    def fetches(i):
        cols = pl.ds(i * WIDTH, WIDTH)
        return [
            pltpu.make_async_copy(src.at[:, cols], dst.at[:, cols], sems.at[j, i])
            for j, (src, dst) in enumerate(zip(table_hbm, table_refs))
        ]

    steps = table_hbm[0].shape[1] // WIDTH
    for i in range(steps):
        for fetch in fetches(i):
            fetch.start()
    turned[...] = d_ref[...].astype(f32).T.astype(bf16)
    for i in range(steps):
        for fetch in fetches(i):
            fetch.wait()
        start, term = 0, 0.0
        for t_ref in table_refs:
            stop = start + t_ref.shape[0]
            part = t_ref[:, i * WIDTH : (i + 1) * WIDTH]
            term += jnp.dot(turned[:, start:stop], part, preferred_element_type=f32)
            start = stop
        for j in range(WIDTH // width):
            spot = order[i * (WIDTH // width) + j]
            one, two = spot // 4, spot % 4
            block = term[:, j * width : (j + 1) * width].astype(bf16)
            own_ref[one, :, pl.ds(pl.multiple_of(two * width, width), width)] = block[:tokens]
            their_ref[two, :, pl.ds(pl.multiple_of(one * width, width), width)] = block[tokens:]


def shards(hidden, table, targets, token_scale, enc_ids, enc_cot, dec_ids, dec_cot):
    rows, depth = table.shape
    tokens = hidden.shape[0]
    vocab = rows * NZ
    z, c = lax.axis_index("z"), lax.axis_index("c")
    x, y = lax.axis_index("x"), lax.axis_index("y")
    base = (x * NY + y) * (vocab * 2)

    cots = pl.pallas_call(
        gather_body,
        out_shape=jax.ShapeDtypeStruct((2 * enc_cot.shape[0], depth + 128), bf16),
        compiler_params=ALONE,
        name="id_rows",
    )(enc_ids[None], dec_ids[None], enc_cot, dec_cot)
    cots = lax.all_gather(cots, ("c", "x", "y"), axis=0, tiled=True)
    n_ids = cots.shape[0]
    peers = 2 * NX * NY

    half = rows // 2
    up, down = shift(table, 1), shift(table, -1)
    blocks = {0: table, -1: up, 1: down}
    other, wanted, scales = swap(hidden), swap(targets), swap(token_scale)
    wanted = jnp.concatenate([targets, wanted])[None]
    scales = jnp.concatenate([token_scale, scales])[None]
    for k in range(2, NZ // 2):
        up, down = lax.optimization_barrier((up, down, other, wanted, scales))[:2]
        up, down = shift(up, 1), shift(down, -1)
        blocks[-k], blocks[k] = up, down
    up, down = shift(up[:half], 1), shift(down[half:], -1)
    blocks[NZ // 2] = jnp.concatenate([up, down], 0)

    order = [[0, 1, -1, 2], [-2, 3, -3], [NZ // 2]]
    parts = [jnp.concatenate([blocks[k] for k in g], 0) for g in order]
    parts = [lax.optimization_barrier(part) for part in parts]
    states = jnp.concatenate([hidden, other], 0)
    logits = jnp.concatenate(
        [
            lax.dot_general(g, states, (((1,), (1,)), ((), ())), preferred_element_type=f32)
            for g in parts
        ],
        0,
    )
    places = jnp.array([k for g in order for k in g], i32)
    places = (z + places + NZ) % NZ
    spread = jnp.arange(rows, dtype=i32)
    names = ((base + (places * 2 + c) * rows)[:, None] + spread).reshape(vocab, 1)
    in_order = ((base + (jnp.arange(NZ, dtype=i32) * 2 + c) * rows)[:, None] + spread).reshape(vocab, 1)

    stats = pl.pallas_call(
        stats_body,
        out_shape=jax.ShapeDtypeStruct((peers, 3, 2 * tokens), f32),
        in_specs=[SMEM] + [VMEM] * 3,
        out_specs=VMEM,
        compiler_params=PARAMS,
        cost_estimate=cost(8 * vocab * tokens, 8 * vocab * tokens),
        name="stats",
    )(c.astype(i32)[None], logits, names, wanted)
    stats = lax.all_to_all(stats, ("c", "x", "y"), 0, 0, tiled=True)

    looked_up = pl.pallas_call(
        lookup_body,
        out_shape=jax.ShapeDtypeStruct((vocab, depth), bf16),
        in_specs=[VMEM, ANY],
        out_specs=ANY,
        scratch_shapes=[
            pltpu.VMEM((vocab, n_ids), bf16),
            pltpu.VMEM((n_ids, depth), bf16),
            pltpu.VMEM((n_ids, 128), bf16),
            pltpu.VMEM((2, vocab, WIDTH), bf16),
            pltpu.SemaphoreType.DMA((depth // WIDTH + 1,)),
            pltpu.SemaphoreType.DMA((2,)),
        ],
        compiler_params=ALONE,
        cost_estimate=cost(2 * vocab * n_ids * depth, 2 * n_ids * depth + 2 * vocab * depth),
        name="lookup",
    )(in_order, cots)
    stats, looked_up = lax.optimization_barrier((stats, looked_up))
    row_max = jnp.max(stats[:, 0], axis=0)
    row_sum = jnp.sum(stats[:, 1] * jnp.exp(stats[:, 0] - row_max), axis=0)
    loss = row_max + jnp.log(row_sum) - jnp.sum(stats[:, 2], axis=0)

    head, dlogits = pl.pallas_call(
        head_body,
        out_shape=(
            jax.ShapeDtypeStruct((vocab, depth), bf16),
            jax.ShapeDtypeStruct((vocab, 2 * tokens), bf16),
        ),
        in_specs=[SMEM] + [VMEM] * 4 + [ANY] * 3,
        out_specs=(ANY, VMEM),
        scratch_shapes=[
            pltpu.VMEM((vocab, 2 * tokens), bf16),
            pltpu.VMEM((tokens, depth), bf16),
            pltpu.VMEM((tokens, depth), bf16),
            pltpu.VMEM((vocab, depth), bf16),
            pltpu.VMEM((2, vocab, WIDTH), bf16),
            pltpu.SemaphoreType.DMA((3, depth // WIDTH)),
            pltpu.SemaphoreType.DMA((2,)),
        ],
        compiler_params=ALONE,
        cost_estimate=cost(4 * vocab * tokens * depth, 4 * vocab * depth + 4 * tokens * depth),
        name="head",
    )(
        places * rows, logits, names, jnp.concatenate([row_max[None], row_sum[None], scales]),
        wanted, hidden, other, looked_up,
    )
    grad_table = lax.psum_scatter(head, "z", scatter_dimension=0, tiled=True).astype(f32)

    width = depth // (NX * NY)
    spot = jnp.arange(NX * NY, dtype=i32)
    spot = jnp.where(c == 0, spot, spot % 4 * 4 + spot // 4)
    own, theirs = pl.pallas_call(
        state_body,
        out_shape=(jax.ShapeDtypeStruct((4, tokens, depth // 4), bf16),) * 2,
        in_specs=[SMEM, VMEM] + [ANY] * len(parts),
        out_specs=(VMEM, VMEM),
        scratch_shapes=[pltpu.VMEM((2 * tokens, vocab), bf16)]
        + [pltpu.VMEM(part.shape, bf16) for part in parts]
        + [pltpu.SemaphoreType.DMA((len(parts), depth // WIDTH))],
        compiler_params=PARAMS,
        cost_estimate=cost(4 * vocab * tokens * depth, 2 * (vocab + 2 * tokens) * depth),
        name="state_terms",
    )(spot, dlogits, *parts)
    term = (own.astype(f32) + swap(theirs).astype(f32)).astype(bf16)
    term = jnp.sum(exchange(term, 0).astype(f32), 0)
    term = jnp.stack([term[:, i * width : (i + 1) * width] for i in range(4)]).astype(bf16)
    grad_hidden = jnp.sum(exchange(term, 1).astype(f32), 0).astype(bf16)
    return (grad_hidden, grad_table, loss[:tokens])


def solution(mesh):
    fine = Mesh(mesh.devices.reshape(NZ, 2, NX, NY), ("z", "c", "x", "y"))
    dp, vocab, every = ("z", "c"), ("x", "y"), ("z", "c", "x", "y")
    return jax.shard_map(
        shards,
        mesh=fine,
        in_specs=(
            P(dp, None), P(vocab + dp, None), P(dp), P(dp),
            P(every), P(every, None), P(every), P(every, None),
        ),
        out_specs=(P(dp, vocab), P(vocab + dp, None), P(dp)),
        check_vma=False,
    )
```

```python
import jax
import jax.numpy as jnp
from jax import lax
from jax.experimental import pallas as pl
from jax.experimental.pallas import tpu as pltpu
from jax.sharding import Mesh, PartitionSpec as P

bf16, f32, i32 = jnp.bfloat16, jnp.float32, jnp.int32
NX, NY, NZ = 4, 4, 8
PARAMS = pltpu.CompilerParams(vmem_limit_bytes=40 << 20)
ANY = pl.BlockSpec(memory_space=pl.ANY)
VMEM = pl.BlockSpec(memory_space=pltpu.VMEM)
SMEM = pl.BlockSpec(memory_space=pltpu.SMEM)
WIDTH = 512
ALONE = pltpu.CompilerParams(vmem_limit_bytes=60 << 20)


def shift(x, k):
    return lax.ppermute(x, "z", [(i, (i + k) % NZ) for i in range(NZ)])


def swap(x):
    return lax.ppermute(x, "c", [(0, 1), (1, 0)])


def after(x, *others):
    return lax.optimization_barrier((x,) + others)[0]


def legs(leg):
    groups = []
    for c in range(2):
        for i in range(4):
            places = [(j, i) if c == leg else (i, j) for j in range(4)]
            groups.append([(c * NX + x) * NY + y for x, y in places])
    return groups


def exchange(x, leg):
    return lax.all_to_all(
        x, ("c", "x", "y"), 0, 0, axis_index_groups=legs(leg), tiled=True
    )


def cost(flops, moved):
    return pl.CostEstimate(flops=flops, bytes_accessed=moved, transcendentals=0)


def gather_body(enc_ids_ref, dec_ids_ref, enc_ref, dec_ref, out_ref):
    n, depth = enc_ref.shape
    row = lax.broadcasted_iota(i32, (n, n), 0)
    same = row == lax.broadcasted_iota(i32, (n, n), 1)
    lane = lax.broadcasted_iota(i32, (n, 128), 1)
    for i, (ids_ref, rows_ref) in enumerate(((enc_ids_ref, enc_ref), (dec_ids_ref, dec_ref))):
        out_ref[i * n : (i + 1) * n, :depth] = rows_ref[...]
        ids = jnp.sum(jnp.where(same, ids_ref[...], 0), axis=1, keepdims=True)
        tail = jnp.where(lane == 0, ids >> 7, jnp.where(lane == 1, ids & 127, 0))
        out_ref[i * n : (i + 1) * n, depth:] = tail.astype(f32).astype(bf16)


def stats_body(core, logits_ref, names_ref, wanted_ref, out_ref):
    logits = logits_ref[...]
    top = jnp.max(logits, axis=0, keepdims=True)
    total = jnp.sum(jnp.exp(logits - top), axis=0, keepdims=True)
    hit = names_ref[...] == wanted_ref[...]
    target = jnp.sum(jnp.where(hit, logits, 0.0), axis=0, keepdims=True)
    peers, tokens = out_ref.shape[0] // 2, out_ref.shape[2] // 2
    for i, value in enumerate((top, total, target)):
        turned = jnp.concatenate([value[:, tokens:], value[:, :tokens]], 1)
        for c in range(2):
            message = jnp.where(core[0] == c, value, turned)
            for j in range(peers):
                out_ref[c * peers + j, i : i + 1] = message


def columns(ref, i):
    return ref.at[:, pl.ds(i * WIDTH, WIDTH)]


def lookup_body(names_ref, cots_hbm, out_hbm, hits, cots_ref, tail_ref, sums, in_sems, out_sems):
    steps = out_hbm.shape[1] // WIDTH

    def fetch(i):
        return pltpu.make_async_copy(columns(cots_hbm, i), columns(cots_ref, i), in_sems.at[i])

    def store(i):
        return pltpu.make_async_copy(sums.at[i % 2], columns(out_hbm, i), out_sems.at[i % 2])

    tail = pltpu.make_async_copy(
        cots_hbm.at[:, pl.ds(steps * WIDTH, 128)], tail_ref, in_sems.at[steps]
    )
    tail.start()
    for i in range(steps):
        fetch(i).start()
    tail.wait()
    ids = tail_ref[...].astype(f32).T
    ids = ids[0:1] * 128.0 + ids[1:2]
    hits[...] = (names_ref[...].astype(f32) == ids).astype(f32).astype(bf16)
    for i in range(steps):
        fetch(i).wait()
        if i >= 2:
            store(i - 2).wait()
        cols = slice(i * WIDTH, (i + 1) * WIDTH)
        term = jnp.dot(hits[...], cots_ref[:, cols], preferred_element_type=f32)
        sums[i % 2] = term.astype(bf16)
        store(i).start()
    store(steps - 2).wait()
    store(steps - 1).wait()


def head_body(
    starts, logits_ref, names_ref, stats_ref, scale_ref, wanted_ref, own_hbm, other_hbm, looked_hbm,
    out_hbm, d_ref, sorted_ref, own_ref, other_ref, looked_ref, sums, in_sems, out_sems,
):
    steps = out_hbm.shape[1] // WIDTH

    def fetches(i):
        pairs = ((own_hbm, own_ref), (other_hbm, other_ref), (looked_hbm, looked_ref))
        return [
            pltpu.make_async_copy(columns(src, i), columns(dst, i), in_sems.at[j, i])
            for j, (src, dst) in enumerate(pairs)
        ]

    def store(i):
        return pltpu.make_async_copy(sums.at[i % 2], columns(out_hbm, i), out_sems.at[i % 2])

    for i in range(steps):
        for fetch in fetches(i):
            fetch.start()
    tops = stats_ref[:, 0, :]
    top = jnp.max(tops, axis=0, keepdims=True)
    total = jnp.sum(stats_ref[:, 1, :] * jnp.exp(tops - top), axis=0, keepdims=True)
    share = jnp.exp(logits_ref[...] - top) * (1.0 / total)
    hit = (names_ref[...] == wanted_ref[...]).astype(f32)
    d_ref[...] = (scale_ref[...] * (share - hit)).astype(bf16)
    pieces = starts.shape[0]
    rows = d_ref.shape[0] // pieces
    for k in range(pieces):
        start = pl.multiple_of(starts[k], rows)
        sorted_ref[pl.ds(start, rows), :] = d_ref[k * rows : (k + 1) * rows]

    tokens = own_ref.shape[0]
    for i in range(steps):
        for fetch in fetches(i):
            fetch.wait()
        cols = slice(i * WIDTH, (i + 1) * WIDTH)
        term = looked_ref[:, cols].astype(f32)
        term += jnp.dot(sorted_ref[:, :tokens], own_ref[:, cols], preferred_element_type=f32)
        term += jnp.dot(sorted_ref[:, tokens:], other_ref[:, cols], preferred_element_type=f32)
        if i >= 2:
            store(i - 2).wait()
        sums[i % 2] = term.astype(bf16)
        store(i).start()
    store(steps - 2).wait()
    store(steps - 1).wait()


def state_body(order, d_ref, *refs):
    n = (len(refs) - 4) // 2
    table_hbm, own_ref, their_ref, turned = refs[:n], refs[n], refs[n + 1], refs[n + 2]
    table_refs, sems = refs[n + 3 : -1], refs[-1]
    tokens, width = own_ref.shape[1], own_ref.shape[2] // 4

    def fetches(i):
        cols = pl.ds(i * WIDTH, WIDTH)
        return [
            pltpu.make_async_copy(src.at[:, cols], dst.at[:, cols], sems.at[j, i])
            for j, (src, dst) in enumerate(zip(table_hbm, table_refs))
        ]

    steps = table_hbm[0].shape[1] // WIDTH
    for i in range(steps):
        for fetch in fetches(i):
            fetch.start()
    turned[...] = d_ref[...].astype(f32).T.astype(bf16)
    for i in range(steps):
        for fetch in fetches(i):
            fetch.wait()
        start, term = 0, 0.0
        for t_ref in table_refs:
            stop = start + t_ref.shape[0]
            part = t_ref[:, i * WIDTH : (i + 1) * WIDTH]
            term += jnp.dot(turned[:, start:stop], part, preferred_element_type=f32)
            start = stop
        for j in range(WIDTH // width):
            spot = order[i * (WIDTH // width) + j]
            one, two = spot // 4, spot % 4
            block = term[:, j * width : (j + 1) * width].astype(bf16)
            own_ref[one, :, pl.ds(pl.multiple_of(two * width, width), width)] = block[:tokens]
            their_ref[two, :, pl.ds(pl.multiple_of(one * width, width), width)] = block[tokens:]


def shards(hidden, table, targets, token_scale, enc_ids, enc_cot, dec_ids, dec_cot):
    rows, depth = table.shape
    tokens = hidden.shape[0]
    vocab = rows * NZ
    z, c = lax.axis_index("z"), lax.axis_index("c")
    x, y = lax.axis_index("x"), lax.axis_index("y")
    base = (x * NY + y) * (vocab * 2)

    cots = pl.pallas_call(
        gather_body,
        out_shape=jax.ShapeDtypeStruct((2 * enc_cot.shape[0], depth + 128), bf16),
        compiler_params=ALONE,
        name="id_rows",
    )(enc_ids[None], dec_ids[None], enc_cot, dec_cot)
    cots = lax.all_gather(cots, ("c", "x", "y"), axis=0, tiled=True)
    n_ids = cots.shape[0]
    peers = 2 * NX * NY

    half = rows // 2
    up, down = shift(table, 1), shift(table, -1)
    blocks = {0: table, -1: up, 1: down}
    other, wanted, scales = swap(hidden), swap(targets), swap(token_scale)
    wanted = jnp.concatenate([targets, wanted])[None]
    scales = jnp.concatenate([token_scale, scales])[None]
    for k in range(2, NZ // 2):
        up, down = lax.optimization_barrier((up, down, other, wanted, scales))[:2]
        up, down = shift(up, 1), shift(down, -1)
        blocks[-k], blocks[k] = up, down
    up, down = shift(up[:half], 1), shift(down[half:], -1)
    blocks[NZ // 2] = jnp.concatenate([up, down], 0)

    order = [[0, 1, -1, 2], [-2, 3, -3], [NZ // 2]]
    parts = [jnp.concatenate([blocks[k] for k in g], 0) for g in order]
    parts = [lax.optimization_barrier(part) for part in parts]
    states = jnp.concatenate([hidden, other], 0)
    logits = jnp.concatenate(
        [
            lax.dot_general(g, states, (((1,), (1,)), ((), ())), preferred_element_type=f32)
            for g in parts
        ],
        0,
    )
    places = jnp.array([k for g in order for k in g], i32)
    places = (z + places + NZ) % NZ
    spread = jnp.arange(rows, dtype=i32)
    names = ((base + (places * 2 + c) * rows)[:, None] + spread).reshape(vocab, 1)
    in_order = ((base + (jnp.arange(NZ, dtype=i32) * 2 + c) * rows)[:, None] + spread).reshape(vocab, 1)

    stats = pl.pallas_call(
        stats_body,
        out_shape=jax.ShapeDtypeStruct((peers, 3, 2 * tokens), f32),
        in_specs=[SMEM] + [VMEM] * 3,
        out_specs=VMEM,
        compiler_params=PARAMS,
        cost_estimate=cost(8 * vocab * tokens, 8 * vocab * tokens),
        name="stats",
    )(c.astype(i32)[None], logits, names, wanted)
    stats = lax.all_to_all(stats, ("c", "x", "y"), 0, 0, tiled=True)

    looked_up = pl.pallas_call(
        lookup_body,
        out_shape=jax.ShapeDtypeStruct((vocab, depth), bf16),
        in_specs=[VMEM, ANY],
        out_specs=ANY,
        scratch_shapes=[
            pltpu.VMEM((vocab, n_ids), bf16),
            pltpu.VMEM((n_ids, depth), bf16),
            pltpu.VMEM((n_ids, 128), bf16),
            pltpu.VMEM((2, vocab, WIDTH), bf16),
            pltpu.SemaphoreType.DMA((depth // WIDTH + 1,)),
            pltpu.SemaphoreType.DMA((2,)),
        ],
        compiler_params=ALONE,
        cost_estimate=cost(2 * vocab * n_ids * depth, 2 * n_ids * depth + 2 * vocab * depth),
        name="lookup",
    )(in_order, cots)
    stats, looked_up = lax.optimization_barrier((stats, looked_up))
    row_max = jnp.max(stats[:, 0], axis=0)
    row_sum = jnp.sum(stats[:, 1] * jnp.exp(stats[:, 0] - row_max), axis=0)
    loss = row_max + jnp.log(row_sum) - jnp.sum(stats[:, 2], axis=0)

    head, dlogits = pl.pallas_call(
        head_body,
        out_shape=(
            jax.ShapeDtypeStruct((vocab, depth), bf16),
            jax.ShapeDtypeStruct((vocab, 2 * tokens), bf16),
        ),
        in_specs=[SMEM] + [VMEM] * 5 + [ANY] * 3,
        out_specs=(ANY, VMEM),
        scratch_shapes=[
            pltpu.VMEM((vocab, 2 * tokens), bf16),
            pltpu.VMEM((tokens, depth), bf16),
            pltpu.VMEM((tokens, depth), bf16),
            pltpu.VMEM((vocab, depth), bf16),
            pltpu.VMEM((2, vocab, WIDTH), bf16),
            pltpu.SemaphoreType.DMA((3, depth // WIDTH)),
            pltpu.SemaphoreType.DMA((2,)),
        ],
        compiler_params=ALONE,
        cost_estimate=cost(4 * vocab * tokens * depth, 4 * vocab * depth + 4 * tokens * depth),
        name="head",
    )(
        places * rows, logits, names, stats, scales,
        wanted, hidden, other, looked_up,
    )
    grad_table = lax.psum_scatter(head, "z", scatter_dimension=0, tiled=True).astype(f32)

    width = depth // (NX * NY)
    spot = jnp.arange(NX * NY, dtype=i32)
    spot = jnp.where(c == 0, spot, spot % 4 * 4 + spot // 4)
    own, theirs = pl.pallas_call(
        state_body,
        out_shape=(jax.ShapeDtypeStruct((4, tokens, depth // 4), bf16),) * 2,
        in_specs=[SMEM, VMEM] + [ANY] * len(parts),
        out_specs=(VMEM, VMEM),
        scratch_shapes=[pltpu.VMEM((2 * tokens, vocab), bf16)]
        + [pltpu.VMEM(part.shape, bf16) for part in parts]
        + [pltpu.SemaphoreType.DMA((len(parts), depth // WIDTH))],
        compiler_params=PARAMS,
        cost_estimate=cost(4 * vocab * tokens * depth, 2 * (vocab + 2 * tokens) * depth),
        name="state_terms",
    )(spot, dlogits, *parts)
    term = (own.astype(f32) + swap(theirs).astype(f32)).astype(bf16)
    term = jnp.sum(exchange(term, 0).astype(f32), 0)
    term = jnp.stack([term[:, i * width : (i + 1) * width] for i in range(4)]).astype(bf16)
    grad_hidden = jnp.sum(exchange(term, 1).astype(f32), 0).astype(bf16)
    return (grad_hidden, grad_table, loss[:tokens])


def solution(mesh):
    fine = Mesh(mesh.devices.reshape(NZ, 2, NX, NY), ("z", "c", "x", "y"))
    dp, vocab, every = ("z", "c"), ("x", "y"), ("z", "c", "x", "y")
    return jax.shard_map(
        shards,
        mesh=fine,
        in_specs=(
            P(dp, None), P(vocab + dp, None), P(dp), P(dp),
            P(every), P(every, None), P(every), P(every, None),
        ),
        out_specs=(P(dp, vocab), P(vocab + dp, None), P(dp)),
        check_vma=False,
    )
```
